512 devices in a mesh: ctx: 16 (over x, z_hi, core), head: 32 (over z_lo, y).
Axes of the slice: x: 4, y: 4, z: 16 (z_hi: 2, z_lo: 8; z = z_hi * 8 + z_lo), core: 2. Of those that a mesh axis runs over, the one named last changes fastest.
Arguments:
- q_nope: bfloat16 [2048, 128, 128], P('ctx', 'head'), may hold values from -6 to 6
- q_rope: bfloat16 [2048, 128, 64], P('ctx', 'head'), may hold values from -300 to 300
- w_uk: bfloat16 [128, 128, 512], P('head'), may hold values from -0.5 to 0.5
- w_uv: bfloat16 [128, 512, 128], P('head'), may hold values from -0.75 to 0.75
- w_o: bfloat16 [16384, 7168], P('head', 'ctx'), may hold values from -0.125 to 0.125
- cache_kv: bfloat16 [2048, 576], P('ctx'), may hold values from -4 to 4
- new_kv: bfloat16 [2048, 576], P('ctx'), may hold values from -4 to 4
- block_order: int32 [16], replicated, may hold values from 0 to 15, each once
- cache_lengths: int32 [16], replicated, may hold values from 32 to 128, as said below
Outputs:
- mixed: bfloat16 [2048, 7168], P(('ctx', 'head'))
The draws below stay inside these ranges and needn't reach their ends.
Inputs may be any that keep to these rules, and one draw needn't show every extreme that they name: `cache_lengths`: at least one ctx index has all 128 slots valid.
All inputs are finite; a program needn't handle non-finite values.
Results may differ from the reference program's by a relative error of at most 0.024.
Values may be sent and summed in bfloat16 or wider, within the bound.
No kernel may reach another device: no remote copies, remote signals or barrier semaphores. Data moves between devices by JAX's collectives and lax.ppermute only.
A program may use at most 64 MiB of HBM per device.

```python
import jax
import jax.numpy as jnp
from jax import lax

D = 7168
LATENT = 512
ROPE = 64
NOPE = 128
VDIM = 128
TQ_DEV = 128
SK_DEV = 128
HEADS = 128
TOKENS = 2048
CACHE = 2048
N_CTX = 16


def base_cache(key):
    values = jax.random.normal(jax.random.fold_in(key, 11), (CACHE, LATENT + ROPE), jnp.float32)
    return jnp.clip(values, -4.0, 4.0)


def draw_cache_kv(key, part):
    values = base_cache(key)
    return values.astype(jnp.bfloat16)


def draw_q_rope(key, part):
    values = jax.random.normal(jax.random.fold_in(key, 23), (TOKENS, HEADS, ROPE), jnp.float32)
    values = jnp.clip(values, -4.0, 4.0)
    return values.astype(jnp.bfloat16)


def draw_cache_lengths(key, part):
    shard_count = CACHE // SK_DEV
    values = jax.random.randint(jax.random.fold_in(key, 5), (shard_count,), SK_DEV // 4, SK_DEV + 1)
    fullest = jax.random.randint(jax.random.fold_in(key, 7), (), 0, shard_count)
    return jnp.where(jnp.arange(shard_count) == fullest, SK_DEV, values).astype(jnp.int32)


def levels(own_key, dims, cuts, smallest, top_value):
    def one(axis_at, parts):
        draws = jax.random.uniform(jax.random.fold_in(jax.random.fold_in(own_key, 6), axis_at), (parts,), jnp.float32, smallest / len(cuts), top_value / len(cuts))
        return jnp.repeat(jnp.exp(draws), dims[axis_at] // parts).reshape((-1,) + (1,) * (len(dims) - axis_at - 1))

    level = one(*cuts[0])
    for cut in cuts[1:]:
        level = level * one(*cut)
    return level


def bell_draw(rng, shape, width, limit, pieces=(), kind=jnp.bfloat16):
    drawn = width * jax.random.normal(rng, shape, jnp.float32)
    if pieces:
        drawn = drawn * levels(rng, shape, pieces, -0.22, 0.18)
    return jnp.clip(drawn, -limit, limit).astype(kind)


def setup_inputs(seed: int = 0) -> dict:
    seeds = jax.random.split(jax.random.key(seed), 10)
    return {
        "q_nope": bell_draw(seeds[0], (TOKENS, HEADS, NOPE), 1.5, 6.0, ((0, 16), (1, 32))),
        "q_rope": draw_q_rope(jax.random.fold_in(seeds[9], 71), 0),
        "w_uk": bell_draw(seeds[2], (HEADS, NOPE, LATENT), NOPE ** -0.5, 0.5, ((0, 32),)),
        "w_uv": bell_draw(seeds[3], (HEADS, LATENT, VDIM), (LATENT // 8) ** -0.5, 0.75, ((0, 32),)),
        "w_o": bell_draw(seeds[4], (HEADS * VDIM, D), (HEADS * VDIM // 8) ** -0.5, 0.125, ((0, 32), (1, 16))),
        "cache_kv": draw_cache_kv(jax.random.fold_in(seeds[9], 71), 0),
        "new_kv": bell_draw(seeds[6], (TOKENS, LATENT + ROPE), 1.0, 4.0, ((0, 16),)),
        "block_order": jax.random.permutation(seeds[7], N_CTX).astype(jnp.int32),
        "cache_lengths": draw_cache_lengths(jax.random.fold_in(seeds[9], 71), 0),
    }


neg_large = -1.0e30


def reference(q_nope, q_rope, w_uk, w_uv, w_o, cache_kv, new_kv, block_order, cache_lengths):
    score_scale = float(NOPE + ROPE) ** -0.5
    token_ids = jnp.arange(TOKENS, dtype=jnp.int32)
    query_pos = block_order[token_ids // TQ_DEV] * TQ_DEV + token_ids % TQ_DEV
    slot_ids = jnp.arange(CACHE, dtype=jnp.int32)
    cache_valid = (slot_ids % SK_DEV) < cache_lengths[slot_ids // SK_DEV]
    visible = jnp.concatenate(
        [jnp.broadcast_to(cache_valid[None, :], (TOKENS, CACHE)), query_pos[None, :] <= query_pos[:, None]], axis=1)
    all_keys = jnp.concatenate([cache_kv, new_kv], axis=0)
    key_latent = all_keys[:, :LATENT]

    def one_head(inputs):
        nope_part, rope_part, up_key, up_value = inputs
        latent_query = jnp.dot(nope_part, up_key, preferred_element_type=jnp.float32)
        query = jnp.concatenate([latent_query, rope_part.astype(jnp.float32)], axis=1).astype(jnp.bfloat16)
        scores = lax.dot_general(query, all_keys, (((1,), (1,)), ((), ())),
                                 preferred_element_type=jnp.float32) * score_scale
        highest = jnp.max(jnp.where(visible, scores, neg_large), axis=1)
        expo = jnp.where(visible, jnp.exp(scores - highest[:, None]), 0.0)
        totals = jnp.sum(expo, axis=1)
        weighted = jnp.dot(expo.astype(jnp.bfloat16), key_latent, preferred_element_type=jnp.float32)
        latent_out = (weighted / totals[:, None]).astype(jnp.bfloat16)
        return jnp.dot(latent_out, up_value, preferred_element_type=jnp.float32).astype(jnp.bfloat16)

    head_out = lax.map(one_head, (jnp.transpose(q_nope, (1, 0, 2)), jnp.transpose(q_rope, (1, 0, 2)), w_uk, w_uv))
    flat_out = jnp.transpose(head_out, (1, 0, 2)).reshape(TOKENS, HEADS * VDIM)
    return jnp.dot(flat_out, w_o, preferred_element_type=jnp.float32).astype(jnp.bfloat16)
```

```python
import jax
import jax.numpy as jnp
from jax import lax
from jax.sharding import Mesh
from jax.sharding import PartitionSpec as P

neg_large = -1e30
f32 = jnp.float32
bf16 = jnp.bfloat16


def spread(value, axes):
    count = lax.axis_size(axes)
    copies = jnp.broadcast_to(value[None], (count,) + value.shape)
    return lax.all_to_all(copies, axes, 0, 0, tiled=False)


def on_device(q_nope, q_rope, w_uk, w_uv, w_o, cache_kv, new_kv, block_order, cache_lengths):
    tok_rows, heads_here, nope_width = q_nope.shape
    latent_width = w_uk.shape[2]
    value_width = w_uv.shape[2]
    key_width = cache_kv.shape[1]
    cache_rows = cache_kv.shape[0]
    shard_rows = cache_rows + tok_rows
    x_size, zh_size, core_size = (lax.axis_size(a) for a in ("x", "zh", "core"))
    zl_size, y_size = lax.axis_size("zl"), lax.axis_size("y")
    x_at, zh_at, core_at, zl_at, y_at = (lax.axis_index(a) for a in ("x", "zh", "core", "zl", "y"))
    score_scale = float(nope_width + q_rope.shape[2]) ** (-0.5)
    query_rows = tok_rows * heads_here

    swap_zh = [(0, 1), (1, 0)]
    mirror = [(i, zh_size * zl_size - 1 - i) for i in range(zh_size * zl_size)]

    local_keys = jnp.concatenate([cache_kv, new_kv], axis=0)
    quarter_rows = shard_rows // y_size
    quarter = lax.dynamic_slice_in_dim(local_keys, y_at * quarter_rows, quarter_rows, 0)
    far_quarter = lax.ppermute(quarter, ("zh", "zl"), mirror)

    value_rows, col_count = w_o.shape
    cols = col_count // y_size
    w_t = w_o.T.reshape(y_size, cols, value_rows)
    w_t = lax.all_to_all(w_t, "y", 0, 0, tiled=False)
    w_t = jnp.transpose(w_t, (1, 0, 2))

    near = spread(local_keys, "x")
    far = spread(far_quarter, ("x", "y"))
    far = far.reshape(x_size, shard_rows, key_width)
    w_far = lax.ppermute(w_t, "zh", swap_zh)
    half = jnp.stack([near, far])
    other_half = lax.ppermute(half, "core", swap_zh)
    piece = jnp.stack([half, other_half])
    piece = piece.reshape(-1, key_width)

    w_pair = jnp.where(zh_at == 0, jnp.stack([w_t, w_far]), jnp.stack([w_far, w_t]))
    w_pair_other = lax.ppermute(w_pair, "core", swap_zh)
    w_all = jnp.where(
        core_at == 0,
        jnp.stack([w_pair, w_pair_other], axis=1),
        jnp.stack([w_pair_other, w_pair], axis=1),
    )
    w_all = w_all.reshape(zh_size * core_size * cols, y_size * value_rows)

    q_latent = jnp.einsum("thn,hnc->thc", q_nope, w_uk, preferred_element_type=f32)
    query = jnp.concatenate([q_latent, q_rope.astype(f32)], axis=2).astype(bf16)
    query = query.reshape(query_rows, query.shape[2])
    ctx_count = x_size * zh_size * core_size
    shard_ids = jnp.arange(ctx_count, dtype=jnp.int32)
    own_ctx = (x_at * zh_size + zh_at) * core_size + core_at
    own_block = jnp.sum(jnp.where(shard_ids == own_ctx, block_order, 0))
    query_pos = own_block * tok_rows + jnp.arange(query_rows, dtype=jnp.int32) // heads_here

    global_rows = jnp.arange(piece.shape[0], dtype=jnp.int32)
    part = global_rows // shard_rows
    offsets = global_rows % shard_rows
    part_x = part % x_size
    part_zh = (part // x_size % zh_size) ^ zh_at
    part_core = (part // (x_size * zh_size)) ^ core_at
    owners = (part_x * zh_size + part_zh) * core_size + part_core
    matches = owners[:, None] == shard_ids[None, :]
    lengths = jnp.sum(jnp.where(matches, cache_lengths[None, :], 0), axis=1)
    blocks = jnp.sum(jnp.where(matches, block_order[None, :], 0), axis=1)
    key_pos = blocks * tok_rows + offsets - cache_rows
    visible = jnp.where(
        (offsets < cache_rows)[None, :],
        (offsets < lengths)[None, :],
        key_pos[None, :] <= query_pos[:, None],
    )
    scores = (
        lax.dot_general(query, piece, (((1,), (1,)), ((), ())), preferred_element_type=f32)
        * score_scale
    )
    best = jnp.max(jnp.where(visible, scores, neg_large), axis=1)
    expo = jnp.where(visible, jnp.exp(scores - best[:, None]), 0.0)
    totals = jnp.sum(expo, axis=1)
    accum = jnp.dot(expo.astype(bf16), piece[:, :latent_width], preferred_element_type=f32)
    latent_out = (accum / totals[:, None]).astype(bf16).reshape(tok_rows, heads_here, latent_width)
    head_out = jnp.einsum("thc,hcv->thv", latent_out, w_uv, preferred_element_type=f32)
    head_out = head_out.astype(bf16).reshape(tok_rows, heads_here * value_width)

    gathered = spread(head_out, ("x", "y"))
    gathered = gathered.reshape(x_size, y_size, zl_size, tok_rows // zl_size, value_rows)
    lhs = jnp.transpose(gathered, (2, 0, 3, 1, 4)).reshape(x_size * tok_rows, y_size * value_rows)
    partial = lax.dot_general(lhs, w_all, (((1,), (1,)), ((), ())), preferred_element_type=f32)
    partial = partial.astype(bf16)

    step = 1
    pieces = partial.reshape(2, 2, 2, -1, partial.shape[1])
    for axis, bit in ((2, 1), (1, 2), (0, 4)):
        mine = (zl_at // bit) % 2
        keep = lax.dynamic_index_in_dim(pieces, mine, axis, keepdims=True)
        send = lax.dynamic_index_in_dim(pieces, 1 - mine, axis, keepdims=True)
        got = lax.ppermute(send, "zl", [(i, i ^ bit) for i in range(zl_size)])
        pieces = (keep.astype(f32) + got.astype(f32)).astype(bf16)
    rows_out = tok_rows // (zl_size * y_size)
    summed = pieces.reshape(x_size * y_size, rows_out, partial.shape[1])
    mixed = lax.all_to_all(summed, ("x", "y"), 0, 0, tiled=False)
    mixed = mixed.reshape(x_size, y_size, rows_out, zh_size * core_size, cols)
    mixed = jnp.transpose(mixed, (2, 0, 3, 1, 4))
    return mixed.reshape(rows_out, x_size * zh_size * core_size * y_size * cols)


def solution(mesh):
    axes = ("x", "zh", "core", "zl", "y")
    fine = Mesh(mesh.devices.reshape(4, 2, 2, 8, 4), axes)
    ctx, head = axes[:3], axes[3:]
    in_specs = (
        P(ctx, head, None),
        P(ctx, head, None),
        P(head, None, None),
        P(head, None, None),
        P(head, ctx),
        P(ctx, None),
        P(ctx, None),
        P(),
        P(),
    )
    out_specs = P(axes, None)
    return jax.shard_map(
        on_device, mesh=fine, in_specs=in_specs, out_specs=out_specs, check_vma=False
    )
```

```python
import functools

import jax
import jax.numpy as jnp
from jax import lax
from jax.experimental import pallas as pl
from jax.experimental.pallas import tpu as pltpu
from jax.sharding import Mesh
from jax.sharding import PartitionSpec as P


neg_large = -1e30
f32 = jnp.float32
bf16 = jnp.bfloat16
swap = ((0, 1), (1, 0))
VMEM = pl.BlockSpec(memory_space=pltpu.VMEM)
SMEM = pl.BlockSpec(memory_space=pltpu.SMEM)


def spread(value, axes):
    count = lax.axis_size(axes)
    copies = jnp.broadcast_to(value[None], (count,) + value.shape)
    return lax.all_to_all(copies, axes, 0, 0, tiled=False)


def cost(flops, nbytes, trans=0):
    return pl.CostEstimate(flops=flops, bytes_accessed=nbytes, transcendentals=trans)


def pack_body(latent_width, cache_ref, new_ref, out_ref):
    rope = cache_ref.shape[1] - latent_width
    for copy in range(out_ref.shape[0]):
        out_ref[copy, :, :latent_width] = cache_ref[:, :latent_width]
        out_ref[copy, :, latent_width : 2 * latent_width] = new_ref[:, :latent_width]
        out_ref[copy, :, 2 * latent_width : 2 * latent_width + rope] = cache_ref[:, latent_width:]
        out_ref[copy, :, 2 * latent_width + rope :] = new_ref[:, latent_width:]


def pack(cache, new, latent_width, copies):
    rows = cache.shape[0]
    shape = (copies, rows, 2 * cache.shape[1])
    return pl.pallas_call(
        functools.partial(pack_body, latent_width),
        out_shape=jax.ShapeDtypeStruct(shape, bf16),
        in_specs=[VMEM, VMEM],
        out_specs=VMEM,
        cost_estimate=cost(0, 4 * shape[0] * shape[1] * shape[2]),
        name="pack",
    )(cache, new)


def attend_body(first, last, pieces, scale, *refs):
    refs = list(refs)
    ql_ref, qr_ref, limit_ref, where_ref = refs[:4]
    keys = refs[4 : 4 + pieces]
    refs = refs[4 + pieces :]
    if not first:
        m_in, l_in, acc_in = refs[:3]
        refs = refs[3:]
    if last:
        wuv_ref = refs[0]
        refs = refs[1:]
    heads, toks, width = ql_ref.shape
    part = keys[0].shape[0] * keys[0].shape[1]
    slots = lax.broadcasted_iota(jnp.int32, (toks, part), 1) % keys[0].shape[1]
    tok = lax.broadcasted_iota(jnp.int32, (toks, part), 0)
    nt = (((1,), (1,)), ((), ()))
    seen_cache = [slots < limit_ref[p : p + 1, :] for p in range(pieces)]
    seen_new = [where_ref[p : p + 1, :] + slots <= tok for p in range(pieces)]
    for h in range(heads):
        scores = []
        for p in range(pieces):
            rope = keys[p][:, :, 2 * width :].reshape(part, -1)
            for kind in range(2):
                lat = keys[p][:, :, kind * width : (kind + 1) * width].reshape(part, width)
                s = lax.dot_general(ql_ref[h], lat, nt, preferred_element_type=f32)
                s = s + lax.dot_general(qr_ref[kind, h], rope, nt, preferred_element_type=f32)
                seen = seen_new[p] if kind else seen_cache[p]
                scores.append(jnp.where(seen, s, neg_large))
        top = functools.reduce(jnp.maximum, scores)
        top = jnp.max(top, axis=1, keepdims=True)
        if first:
            m = top
            total = jnp.zeros((toks, 1), f32)
            acc = None
        else:
            m_old = m_in[h][:, :1]
            m = jnp.maximum(top, m_old)
            keep = jnp.exp2((m_old - m) * scale)
            total = l_in[h][:, :1] * keep
            acc = acc_in[h] * keep
        at = 0
        for p in range(pieces):
            for kind in range(2):
                lat = keys[p][:, :, kind * width : (kind + 1) * width].reshape(part, width)
                e = jnp.exp2((scores[at] - m) * scale)
                at += 1
                total = total + jnp.sum(e, axis=1, keepdims=True)
                d = jnp.dot(e.astype(bf16), lat, preferred_element_type=f32)
                acc = d if acc is None else acc + d
        if last:
            out = (acc / total).astype(bf16)
            wide = jnp.dot(out, wuv_ref[h], preferred_element_type=f32)
            refs[0][:, h * wide.shape[1] : (h + 1) * wide.shape[1]] = wide.astype(bf16)
        else:
            refs[0][h] = jnp.broadcast_to(m, (toks, 128))
            refs[1][h] = jnp.broadcast_to(total, (toks, 128))
            refs[2][h] = acc


def attend(ql, qr, limits, where, keys, scale, state=None, w_uv=None):
    heads, toks, width = ql.shape
    first, last = state is None, w_uv is not None
    args = [ql, qr, limits, where, *keys]
    if not first:
        args += list(state)
    if last:
        args.append(w_uv)
        out_shape = jax.ShapeDtypeStruct((toks, heads * w_uv.shape[2]), bf16)
    else:
        out_shape = (
            jax.ShapeDtypeStruct((heads, toks, 128), f32),
            jax.ShapeDtypeStruct((heads, toks, 128), f32),
            jax.ShapeDtypeStruct((heads, toks, width), f32),
        )
    count = 2 * len(keys) * keys[0].shape[0] * keys[0].shape[1]
    rows = heads * toks
    return pl.pallas_call(
        functools.partial(attend_body, first, last, len(keys), scale),
        out_shape=out_shape,
        in_specs=[VMEM] * len(args),
        out_specs=VMEM if last else (VMEM,) * 3,
        cost_estimate=cost(4 * rows * count * width, 4 * count * width, rows * count),
        name="attend",
    )(*args)


def join_body(flag_ref, near_ref, far_ref, near_other_ref, far_other_ref, out_ref):
    groups, cols = near_ref.shape[0], near_ref.shape[1]
    zh, core, y = flag_ref[0], flag_ref[1], flag_ref[2]
    for ref, a, b in (
        (near_ref, 0, 0),
        (far_ref, 1, 0),
        (near_other_ref, 0, 1),
        (far_other_ref, 1, 1),
    ):
        slot = lax.bitwise_xor(zh, a) * 2 + lax.bitwise_xor(core, b)
        rows = pl.ds(pl.multiple_of(slot * cols, 16), cols)
        for k in range(groups):
            out_ref[lax.rem(y + groups - k, groups), rows, :] = ref[k]


def join(flags, pieces):
    groups, cols, depth = pieces[0].shape
    return pl.pallas_call(
        join_body,
        out_shape=jax.ShapeDtypeStruct((groups, 4 * cols, depth), bf16),
        in_specs=[SMEM] + [VMEM] * 4,
        out_specs=VMEM,
        cost_estimate=cost(0, 16 * groups * cols * depth),
        name="join",
    )(flags, *pieces)


def project_body(zb_size, ho_ref, w_ref, out_ref):
    nt = (((1,), (1,)), ((), ()))
    acc = None
    for y in range(ho_ref.shape[0]):
        d = lax.dot_general(ho_ref[y], w_ref[y], nt, preferred_element_type=f32)
        acc = d if acc is None else acc + d
    acc = acc.astype(bf16)
    rows = out_ref.shape[3]
    for za in range(out_ref.shape[1]):
        for zb in range(zb_size):
            at = (za * zb_size + zb) * rows
            out_ref[zb, za, 0] = acc[at : at + rows]


def project(ho, w, x_size, za_size, zb_size):
    members, toks, depth = ho.shape
    y_size, cols = w.shape[0], w.shape[1]
    rows = toks // (za_size * zb_size)
    return pl.pallas_call(
        functools.partial(project_body, zb_size),
        grid=(x_size,),
        out_shape=jax.ShapeDtypeStruct((zb_size, za_size, x_size, rows, cols), bf16),
        in_specs=[
            pl.BlockSpec((y_size, toks, depth), lambda x: (x, 0, 0)),
            pl.BlockSpec((y_size, cols, depth), lambda x: (0, 0, 0)),
        ],
        out_specs=pl.BlockSpec((zb_size, za_size, 1, rows, cols), lambda x: (0, 0, x, 0, 0)),
        cost_estimate=cost(2 * members * toks * depth * cols, 2 * members * toks * depth),
        name="project",
    )(ho, w)


def layer(q_nope, q_rope, w_uk, w_uv, w_o, cache_kv, new_kv, block_order, cache_lengths):
    tok_rows, _, nope_width = q_nope.shape
    latent_width = w_uk.shape[2]
    x_size, zh_size, core_size, za_size, zb_size, y_size = (
        lax.axis_size(a) for a in ("x", "zh", "core", "za", "zb", "y")
    )
    x_at, zh_at, core_at, y_at = (lax.axis_index(a) for a in ("x", "zh", "core", "y"))
    scale = float(nope_width + q_rope.shape[2]) ** (-0.5) * 1.4426950408889634

    quarter_rows = tok_rows // y_size
    start = y_at * quarter_rows
    quarter = pack(
        lax.dynamic_slice_in_dim(cache_kv, start, quarter_rows, 0),
        lax.dynamic_slice_in_dim(new_kv, start, quarter_rows, 0),
        latent_width,
        1,
    )[0]
    line = zh_size * za_size * zb_size
    mirror = [(i, line - 1 - i) for i in range(line)]
    far_quarter = lax.ppermute(quarter, ("zh", "za", "zb"), mirror)

    value_rows, col_count = w_o.shape
    cols = col_count // y_size
    w_t = w_o.T.reshape(y_size, cols, value_rows)
    parts = [lax.dynamic_index_in_dim(w_t, y_at, 0)]
    for k in range(1, y_size):
        part = lax.dynamic_index_in_dim(w_t, (y_at + k) % y_size, 0)
        parts.append(lax.ppermute(part, "y", [(i, (i + k) % y_size) for i in range(y_size)]))
    w_t = jnp.concatenate(parts, axis=0)
    copies = pack(cache_kv, new_kv, latent_width, x_size)
    near = lax.all_to_all(copies, "x", 0, 0, tiled=False)
    far = spread(far_quarter, ("x", "y"))
    far = far.reshape(x_size, tok_rows, -1)
    w_far = lax.ppermute(w_t, "zh", swap)
    near_other = lax.ppermute(near, "core", swap)
    far_other = lax.ppermute(far, "core", swap)
    w_other = lax.ppermute(w_t, "core", swap)
    w_far_other = lax.ppermute(w_far, "core", swap)

    ql = jnp.einsum("thn,hnc->htc", q_nope, w_uk, preferred_element_type=f32).astype(bf16)
    rope = jnp.transpose(q_rope, (1, 0, 2))
    blank = jnp.zeros_like(rope)
    qr = jnp.stack([jnp.concatenate([rope, blank], axis=2), jnp.concatenate([blank, rope], axis=2)])
    ctx_count = x_size * zh_size * core_size
    shard_ids = jnp.arange(ctx_count, dtype=jnp.int32)
    own_ctx = (x_at * zh_size + zh_at) * core_size + core_at
    own_block = jnp.sum(jnp.where(shard_ids == own_ctx, block_order, 0))

    def of_piece(zh_flip, core_flip):
        column = jnp.arange(x_size * tok_rows, dtype=jnp.int32) // tok_rows
        owner = (column * zh_size + (zh_at ^ zh_flip)) * core_size + (core_at ^ core_flip)
        hit = owner[:, None] == shard_ids[None, :]
        limit = jnp.sum(jnp.where(hit, cache_lengths[None, :], 0), axis=1)
        block = jnp.sum(jnp.where(hit, block_order[None, :], 0), axis=1)
        return limit, (block - own_block) * tok_rows

    tables = [of_piece(a, b) for a in range(2) for b in range(2)]
    limits = jnp.stack([t[0] for t in tables])
    where = jnp.stack([t[1] for t in tables])

    state = attend(ql, qr, limits[:2], where[:2], (near, near_other), scale)
    state = attend(ql, qr, limits[2:3], where[2:3], (far,), scale, state)
    head_out = attend(ql, qr, limits[3:], where[3:], (far_other,), scale, state, w_uv)

    gathered = spread(head_out, ("x", "y"))
    flags = jnp.stack([zh_at, core_at, y_at]).astype(jnp.int32)
    w_all = join(flags, (w_t, w_far, w_other, w_far_other))
    partial = project(gathered, w_all, x_size, za_size, zb_size)

    rows_out = tok_rows // (za_size * zb_size * y_size)
    width = partial.shape[-1]
    partial = partial.reshape(zb_size, -1, width)
    got = lax.all_to_all(partial, "zb", 0, 0, tiled=False)
    partial = jnp.sum(got.astype(f32), axis=0).astype(bf16)
    partial = partial.reshape(za_size * x_size * y_size, rows_out, width)
    got = lax.all_to_all(partial, ("za", "x", "y"), 0, 0, tiled=False)
    got = got.reshape(za_size, x_size, y_size, rows_out, zh_size * core_size, cols)
    mixed = jnp.sum(got.astype(f32), axis=0).astype(bf16)
    mixed = jnp.transpose(mixed, (2, 0, 3, 1, 4))
    return mixed.reshape(rows_out, -1)


def solution(mesh):
    axes = ("x", "zh", "core", "za", "zb", "y")
    fine = Mesh(mesh.devices.reshape(4, 2, 2, 2, 4, 4), axes)
    ctx, head = axes[:3], axes[3:]
    in_specs = (
        P(ctx, head, None),
        P(ctx, head, None),
        P(head, None, None),
        P(head, None, None),
        P(head, ctx),
        P(ctx, None),
        P(ctx, None),
        P(),
        P(),
    )
    out_specs = P(axes, None)
    return jax.shard_map(layer, mesh=fine, in_specs=in_specs, out_specs=out_specs, check_vma=False)
```

```python
import functools

import jax
import jax.numpy as jnp
from jax import lax
from jax.experimental import pallas as pl
from jax.experimental.pallas import tpu as pltpu
from jax.sharding import Mesh
from jax.sharding import PartitionSpec as P


neg_large = -1e30
f32 = jnp.float32
bf16 = jnp.bfloat16
swap = ((0, 1), (1, 0))
VMEM = pl.BlockSpec(memory_space=pltpu.VMEM)
SMEM = pl.BlockSpec(memory_space=pltpu.SMEM)


def spread(value, axes):
    count = lax.axis_size(axes)
    copies = jnp.broadcast_to(value[None], (count,) + value.shape)
    return lax.all_to_all(copies, axes, 0, 0, tiled=False)


def grant(mib):
    return pltpu.CompilerParams(vmem_limit_bytes=mib << 20)


def cost(flops, nbytes, trans=0):
    return pl.CostEstimate(flops=flops, bytes_accessed=nbytes, transcendentals=trans)


def pack_body(latent_width, at_ref, cache_ref, new_ref, copies_ref, part_ref, row_ref):
    rope = cache_ref.shape[0] - latent_width
    row_ref[:latent_width] = cache_ref[:latent_width]
    row_ref[latent_width : 2 * latent_width] = new_ref[:latent_width]
    row_ref[2 * latent_width : 2 * latent_width + rope] = cache_ref[latent_width:]
    row_ref[2 * latent_width + rope :] = new_ref[latent_width:]
    rows = part_ref.shape[0]
    part_ref[...] = row_ref[pl.ds(pl.multiple_of(at_ref[0] * rows, 16), rows), :]
    for copy in range(copies_ref.shape[0]):
        copies_ref[copy] = row_ref[...]


def pack(cache, new, latent_width, copies, part, parts):
    width, slots = cache.shape
    depth = 2 * width
    return pl.pallas_call(
        functools.partial(pack_body, latent_width),
        out_shape=(
            jax.ShapeDtypeStruct((copies, depth, slots), bf16),
            jax.ShapeDtypeStruct((depth // parts, slots), bf16),
        ),
        in_specs=[SMEM, VMEM, VMEM],
        out_specs=(VMEM, VMEM),
        scratch_shapes=[pltpu.VMEM((depth, slots), bf16)],
        cost_estimate=cost(0, 2 * (copies + 2) * depth * slots),
        compiler_params=grant(6),
        name="pack",
    )(part.astype(jnp.int32).reshape(1), cache, new)


def attend_body(first, last, pieces, heads, scale, *refs):
    refs = list(refs)
    ql_ref, qr_ref, limit_ref, where_ref = refs[:4]
    keys = refs[4 : 4 + pieces]
    refs = refs[4 + pieces :]
    if not first:
        m_in, l_in, acc_in = refs[:3]
        refs = refs[3:]
    if last:
        wuv_ref = refs[0]
        refs = refs[1:]
    rows, width = ql_ref.shape
    toks = rows // heads
    shards, depth, slots = keys[0].shape
    part = shards * slots
    slot = lax.broadcasted_iota(jnp.int32, (1, part), 1) % slots
    tok = lax.broadcasted_iota(jnp.int32, (rows, 1), 0) % toks

    def features(p, start, stop):
        return jnp.concatenate([keys[p][s, start:stop, :] for s in range(shards)], axis=1)

    scores = []
    for p in range(pieces):
        rope = features(p, 2 * width, depth)
        for kind in range(2):
            lat = features(p, kind * width, (kind + 1) * width)
            s = jnp.dot(ql_ref[...], lat, preferred_element_type=f32)
            s = s + jnp.dot(qr_ref[kind], rope, preferred_element_type=f32)
            if kind:
                seen = where_ref[p : p + 1, :] + slot <= tok
            else:
                seen = jnp.broadcast_to(slot < limit_ref[p : p + 1, :], s.shape)
            scores.append(jnp.where(seen, s, neg_large))
    top = jnp.max(functools.reduce(jnp.maximum, scores), axis=1, keepdims=True)
    if first:
        m, total, acc = top, None, None
    else:
        m_old = m_in[:, :1]
        m = jnp.maximum(top, m_old)
        keep = jnp.exp2((m_old - m) * scale)
        total = l_in[:, :1] * keep
        acc = acc_in[...] * keep
    sums = None
    for at, s in enumerate(scores):
        p, kind = at // 2, at % 2
        lat = features(p, kind * width, (kind + 1) * width)
        e = jnp.exp2((s - m) * scale)
        sums = e if sums is None else sums + e
        d = lax.dot_general(e.astype(bf16), lat, (((1,), (1,)), ((), ())), preferred_element_type=f32)
        acc = d if acc is None else acc + d
    sums = jnp.sum(sums, axis=1, keepdims=True)
    total = sums if total is None else total + sums
    if last:
        out_ref, hold_ref, sem = refs
        out = (acc / total).astype(bf16)
        value = wuv_ref.shape[2]
        for h in range(heads):
            wide = jnp.dot(
                out[h * toks : (h + 1) * toks], wuv_ref[h], preferred_element_type=f32
            )
            hold_ref[:, h * value : (h + 1) * value] = wide.astype(bf16)
        sends = [
            pltpu.make_async_copy(hold_ref, out_ref.at[c], sem.at[c])
            for c in range(out_ref.shape[0])
        ]
        for send in sends:
            send.start()
        for send in sends:
            send.wait()
    else:
        refs[0][...] = jnp.broadcast_to(m, (rows, 128))
        refs[1][...] = jnp.broadcast_to(total, (rows, 128))
        refs[2][...] = acc


def attend(ql, qr, limits, where, keys, scale, heads, state=None, w_uv=None, copies=0):
    rows, width = ql.shape
    toks = rows // heads
    first, last = state is None, w_uv is not None
    args = [ql, qr, limits, where, *keys]
    scratch = []
    if not first:
        args += list(state)
    if last:
        args.append(w_uv)
        wide = heads * w_uv.shape[2]
        out_shape = jax.ShapeDtypeStruct((copies, toks, wide), bf16)
        scratch = [pltpu.VMEM((toks, wide), bf16), pltpu.SemaphoreType.DMA((copies,))]
    else:
        out_shape = (
            jax.ShapeDtypeStruct((rows, 128), f32),
            jax.ShapeDtypeStruct((rows, 128), f32),
            jax.ShapeDtypeStruct((rows, width), f32),
        )
    count = 2 * len(keys) * keys[0].shape[0] * keys[0].shape[2]
    return pl.pallas_call(
        functools.partial(attend_body, first, last, len(keys), heads, scale),
        out_shape=out_shape,
        in_specs=[VMEM] * len(args),
        out_specs=pl.BlockSpec(memory_space=pltpu.HBM) if last else (VMEM,) * 3,
        scratch_shapes=scratch,
        cost_estimate=cost(4 * rows * count * width, 4 * count * width, rows * count),
        compiler_params=grant(20),
        name="attend",
    )(*args)


def join_body(flag_ref, near_ref, far_ref, near_other_ref, far_other_ref, out_ref):
    groups, cols = near_ref.shape[0], near_ref.shape[1]
    zh, core, y = flag_ref[0], flag_ref[1], flag_ref[2]
    for ref, a, b in (
        (near_ref, 0, 0),
        (far_ref, 1, 0),
        (near_other_ref, 0, 1),
        (far_other_ref, 1, 1),
    ):
        slot = lax.bitwise_xor(zh, a) * 2 + lax.bitwise_xor(core, b)
        rows = pl.ds(pl.multiple_of(slot * cols, 16), cols)
        for k in range(groups):
            out_ref[lax.rem(y + groups - k, groups), rows, :] = ref[k]


def join(flags, pieces):
    groups, cols, depth = pieces[0].shape
    return pl.pallas_call(
        join_body,
        out_shape=jax.ShapeDtypeStruct((groups, 4 * cols, depth), bf16),
        in_specs=[SMEM] + [VMEM] * 4,
        out_specs=VMEM,
        cost_estimate=cost(0, 16 * groups * cols * depth),
        compiler_params=grant(10),
        name="join",
    )(flags, *pieces)


def project_body(sizes, ho_ref, w_ref, out_ref, lhs_ref):
    x_size, za_size, zb_size = sizes
    y_size, toks = w_ref.shape[0], ho_ref.shape[1]
    rows = toks // (za_size * zb_size)
    acc = None
    for y in range(y_size):
        for zb in range(zb_size):
            for za in range(za_size):
                for x in range(x_size):
                    at = ((zb * za_size + za) * x_size + x) * rows
                    src = (za * zb_size + zb) * rows
                    lhs_ref[at : at + rows] = ho_ref[x * y_size + y, src : src + rows]
        d = lax.dot_general(
            w_ref[y], lhs_ref[...], (((1,), (1,)), ((), ())), preferred_element_type=f32
        )
        acc = d if acc is None else acc + d
    acc = acc.astype(bf16)
    width = out_ref.shape[2]
    for zb in range(zb_size):
        out_ref[zb] = acc[:, zb * width : (zb + 1) * width]


def project(ho, w, x_size, za_size, zb_size):
    members, toks, depth = ho.shape
    cols = w.shape[1]
    lhs_rows = x_size * toks
    return pl.pallas_call(
        functools.partial(project_body, (x_size, za_size, zb_size)),
        out_shape=jax.ShapeDtypeStruct((zb_size, cols, lhs_rows // zb_size), bf16),
        in_specs=[VMEM, VMEM],
        out_specs=VMEM,
        scratch_shapes=[pltpu.VMEM((lhs_rows, depth), bf16)],
        cost_estimate=cost(2 * members * toks * depth * cols, 2 * members * toks * depth),
        compiler_params=grant(12),
        name="project",
    )(ho, w)


def layer(q_nope, q_rope, w_uk, w_uv, w_o, cache_kv, new_kv, block_order, cache_lengths):
    tok_rows, heads_here, nope_width = q_nope.shape
    latent_width = w_uk.shape[2]
    x_size, zh_size, core_size, za_size, zb_size, y_size = (
        lax.axis_size(a) for a in ("x", "zh", "core", "za", "zb", "y")
    )
    x_at, zh_at, core_at, y_at = (lax.axis_index(a) for a in ("x", "zh", "core", "y"))
    scale = float(nope_width + q_rope.shape[2]) ** (-0.5) * 1.4426950408889634

    copies, quarter = pack(cache_kv.T, new_kv.T, latent_width, x_size, y_at, y_size)
    line = zh_size * za_size * zb_size
    mirror = [(i, line - 1 - i) for i in range(line)]
    far_quarter = lax.ppermute(quarter, ("zh", "za", "zb"), mirror)

    value_rows, col_count = w_o.shape
    cols = col_count // y_size
    w_t = w_o.T.reshape(y_size, cols, value_rows)
    parts = [lax.dynamic_index_in_dim(w_t, y_at, 0)]
    for k in range(1, y_size):
        part = lax.dynamic_index_in_dim(w_t, (y_at + k) % y_size, 0)
        parts.append(lax.ppermute(part, "y", [(i, (i + k) % y_size) for i in range(y_size)]))
    w_t = jnp.concatenate(parts, axis=0)
    near = lax.all_to_all(copies, "x", 0, 0, tiled=False)
    far = spread(far_quarter, ("x", "y"))
    far = far.reshape(x_size, -1, tok_rows)
    w_far = lax.ppermute(w_t, "zh", swap)
    near_other = lax.ppermute(near, "core", swap)
    far_other = lax.ppermute(far, "core", swap)
    w_other = lax.ppermute(w_t, "core", swap)
    w_far_other = lax.ppermute(w_far, "core", swap)

    ql = jnp.einsum("thn,hnc->htc", q_nope, w_uk, preferred_element_type=f32).astype(bf16)
    ql = ql.reshape(heads_here * tok_rows, latent_width)
    rope = jnp.transpose(q_rope, (1, 0, 2))
    blank = jnp.zeros_like(rope)
    qr = jnp.stack([jnp.concatenate([rope, blank], axis=2), jnp.concatenate([blank, rope], axis=2)])
    qr = qr.reshape(2, heads_here * tok_rows, -1)
    ctx_count = x_size * zh_size * core_size
    shard_ids = jnp.arange(ctx_count, dtype=jnp.int32)
    own_ctx = (x_at * zh_size + zh_at) * core_size + core_at
    own_block = jnp.sum(jnp.where(shard_ids == own_ctx, block_order, 0))

    def of_piece(zh_flip, core_flip):
        column = jnp.arange(x_size * tok_rows, dtype=jnp.int32) // tok_rows
        owner = (column * zh_size + (zh_at ^ zh_flip)) * core_size + (core_at ^ core_flip)
        hit = owner[:, None] == shard_ids[None, :]
        limit = jnp.sum(jnp.where(hit, cache_lengths[None, :], 0), axis=1)
        block = jnp.sum(jnp.where(hit, block_order[None, :], 0), axis=1)
        return limit, (block - own_block) * tok_rows

    tables = [of_piece(a, b) for a in range(2) for b in range(2)]
    limits = jnp.stack([t[0] for t in tables])
    where = jnp.stack([t[1] for t in tables])

    pair = (near, near_other)
    state = attend(ql, qr, limits[:2], where[:2], pair, scale, heads_here)
    state = attend(ql, qr, limits[2:3], where[2:3], (far,), scale, heads_here, state)
    head_out = attend(
        ql, qr, limits[3:], where[3:], (far_other,), scale, heads_here, state, w_uv, x_size * y_size
    )

    gathered = lax.all_to_all(head_out, ("x", "y"), 0, 0, tiled=False)
    flags = jnp.stack([zh_at, core_at, y_at]).astype(jnp.int32)
    w_all = join(flags, (w_t, w_far, w_other, w_far_other))
    partial = project(gathered, w_all, x_size, za_size, zb_size)

    rows_out = tok_rows // (za_size * zb_size * y_size)
    width = partial.shape[1]
    got = lax.all_to_all(partial, "zb", 0, 0, tiled=False)
    partial = jnp.sum(got.astype(f32), axis=0).astype(bf16).T
    partial = partial.reshape(za_size * x_size * y_size, rows_out, width)
    got = lax.all_to_all(partial, ("za", "x", "y"), 0, 0, tiled=False)
    got = got.reshape(za_size, x_size, y_size, rows_out, zh_size * core_size, cols)
    mixed = jnp.sum(got.astype(f32), axis=0).astype(bf16)
    mixed = jnp.transpose(mixed, (2, 0, 3, 1, 4))
    return mixed.reshape(rows_out, -1)


def solution(mesh):
    axes = ("x", "zh", "core", "za", "zb", "y")
    fine = Mesh(mesh.devices.reshape(4, 2, 2, 2, 4, 4), axes)
    ctx, head = axes[:3], axes[3:]
    in_specs = (
        P(ctx, head, None),
        P(ctx, head, None),
        P(head, None, None),
        P(head, None, None),
        P(head, ctx),
        P(ctx, None),
        P(ctx, None),
        P(),
        P(),
    )
    out_specs = P(axes, None)
    return jax.shard_map(layer, mesh=fine, in_specs=in_specs, out_specs=out_specs, check_vma=False)
```

```python
import functools

import jax
import jax.numpy as jnp
from jax import lax
from jax.experimental import pallas as pl
from jax.experimental.pallas import tpu as pltpu
from jax.sharding import Mesh
from jax.sharding import PartitionSpec as P


neg_large = -1e30
f32 = jnp.float32
bf16 = jnp.bfloat16
swap = ((0, 1), (1, 0))
VMEM = pl.BlockSpec(memory_space=pltpu.VMEM)
SMEM = pl.BlockSpec(memory_space=pltpu.SMEM)


def spread(value, axes):
    count = lax.axis_size(axes)
    copies = jnp.broadcast_to(value[None], (count,) + value.shape)
    return lax.all_to_all(copies, axes, 0, 0, tiled=False)


def grant(mib):
    return pltpu.CompilerParams(vmem_limit_bytes=mib << 20)


def cost(flops, nbytes, trans=0):
    return pl.CostEstimate(flops=flops, bytes_accessed=nbytes, transcendentals=trans)


def pack_body(latent_width, at_ref, cache_ref, new_ref, row_ref, part_ref):
    rope = cache_ref.shape[0] - latent_width
    row_ref[:latent_width] = cache_ref[:latent_width]
    row_ref[latent_width : 2 * latent_width] = new_ref[:latent_width]
    row_ref[2 * latent_width : 2 * latent_width + rope] = cache_ref[latent_width:]
    row_ref[2 * latent_width + rope :] = new_ref[latent_width:]
    rows = part_ref.shape[0]
    part_ref[...] = row_ref[pl.ds(pl.multiple_of(at_ref[0] * rows, 16), rows), :]


def pack(cache, new, latent_width, part, parts):
    width, slots = cache.shape
    depth = 2 * width
    return pl.pallas_call(
        functools.partial(pack_body, latent_width),
        out_shape=(
            jax.ShapeDtypeStruct((depth, slots), bf16),
            jax.ShapeDtypeStruct((depth // parts, slots), bf16),
        ),
        in_specs=[SMEM, VMEM, VMEM],
        out_specs=(VMEM, VMEM),
        cost_estimate=cost(0, 6 * depth * slots),
        compiler_params=grant(6),
        name="pack",
    )(part.astype(jnp.int32).reshape(1), cache, new)


def attend_body(first, last, pieces, heads, scale, *refs):
    refs = list(refs)
    ql_ref, qr_ref, limit_ref, where_ref = refs[:4]
    keys = refs[4 : 4 + pieces]
    refs = refs[4 + pieces :]
    if not first:
        m_in, l_in, acc_in = refs[:3]
        refs = refs[3:]
    if last:
        wuv_ref = refs[0]
        refs = refs[1:]
    rows, width = ql_ref.shape
    toks = rows // heads
    shards, depth, slots = keys[0].shape
    part = shards * slots
    slot = lax.broadcasted_iota(jnp.int32, (1, part), 1) % slots
    tok = lax.broadcasted_iota(jnp.int32, (rows, 1), 0) % toks

    def features(p, start, stop):
        return jnp.concatenate([keys[p][s, start:stop, :] for s in range(shards)], axis=1)

    ms, totals, accs = [], [], []
    for r in range(0, rows, 256):
        rs = slice(r, r + 256)
        scores = []
        for p in range(pieces):
            rope = features(p, 2 * width, depth)
            for kind in range(2):
                lat = features(p, kind * width, (kind + 1) * width)
                s = jnp.dot(ql_ref[rs], lat, preferred_element_type=f32)
                s = s + jnp.dot(qr_ref[kind, rs], rope, preferred_element_type=f32)
                if kind:
                    seen = where_ref[p : p + 1, :] + slot <= tok[rs]
                else:
                    seen = jnp.broadcast_to(slot < limit_ref[p : p + 1, :], s.shape)
                scores.append(jnp.where(seen, s, neg_large))
        top = jnp.max(functools.reduce(jnp.maximum, scores), axis=1, keepdims=True)
        if first:
            m, total, acc = top, None, None
        else:
            m_old = m_in[rs, :1]
            m = jnp.maximum(top, m_old)
            keep = jnp.exp2((m_old - m) * scale)
            total = l_in[rs, :1] * keep
            acc = acc_in[rs] * keep
        sums = None
        for at, s in enumerate(scores):
            p, kind = at // 2, at % 2
            lat = features(p, kind * width, (kind + 1) * width)
            e = jnp.exp2((s - m) * scale)
            sums = e if sums is None else sums + e
            d = lax.dot_general(e.astype(bf16), lat, (((1,), (1,)), ((), ())), preferred_element_type=f32)
            acc = d if acc is None else acc + d
        sums = jnp.sum(sums, axis=1, keepdims=True)
        total = sums if total is None else total + sums
        ms.append(m)
        totals.append(total)
        accs.append(acc)
    m, total, acc = (jnp.concatenate(v, axis=0) for v in (ms, totals, accs))
    if last:
        out_ref, hold_ref, sem = refs
        out = (acc / total).astype(bf16)
        value = wuv_ref.shape[2]
        for h in range(heads):
            wide = jnp.dot(
                out[h * toks : (h + 1) * toks], wuv_ref[h], preferred_element_type=f32
            )
            hold_ref[:, h * value : (h + 1) * value] = wide.astype(bf16)
        sends = [
            pltpu.make_async_copy(hold_ref, out_ref.at[c], sem.at[c])
            for c in range(out_ref.shape[0])
        ]
        for send in sends:
            send.start()
        for send in sends:
            send.wait()
    else:
        refs[0][...] = jnp.broadcast_to(m, (rows, 128))
        refs[1][...] = jnp.broadcast_to(total, (rows, 128))
        refs[2][...] = acc


def attend(ql, qr, limits, where, keys, scale, heads, state=None, w_uv=None, copies=0):
    rows, width = ql.shape
    toks = rows // heads
    first, last = state is None, w_uv is not None
    args = [ql, qr, limits, where, *keys]
    scratch = []
    if not first:
        args += list(state)
    if last:
        args.append(w_uv)
        wide = heads * w_uv.shape[2]
        out_shape = pltpu.HBM((copies, toks, wide), bf16)
        scratch = [pltpu.VMEM((toks, wide), bf16), pltpu.SemaphoreType.DMA((copies,))]
    else:
        out_shape = (
            pltpu.VMEM((rows, 128), f32),
            pltpu.VMEM((rows, 128), f32),
            pltpu.VMEM((rows, width), f32),
        )
    count = 2 * len(keys) * keys[0].shape[0] * keys[0].shape[2]
    return pl.pallas_call(
        functools.partial(attend_body, first, last, len(keys), heads, scale),
        out_shape=out_shape,
        in_specs=[VMEM] * len(args),
        out_specs=pl.BlockSpec(memory_space=pltpu.HBM) if last else (VMEM,) * 3,
        scratch_shapes=scratch,
        cost_estimate=cost(4 * rows * count * width, 4 * count * width, rows * count),
        compiler_params=grant(20),
        name="attend",
    )(*args)


def join_body(flag_ref, near_ref, far_ref, near_other_ref, far_other_ref, out_ref):
    cols = near_ref.shape[1]
    zh, core = flag_ref[0], flag_ref[1]
    for ref, a, b in (
        (near_ref, 0, 0),
        (far_ref, 1, 0),
        (near_other_ref, 0, 1),
        (far_other_ref, 1, 1),
    ):
        slot = lax.bitwise_xor(zh, a) * 2 + lax.bitwise_xor(core, b)
        rows = pl.ds(pl.multiple_of(slot * cols, 16), cols)
        out_ref[:, rows, :] = ref[...]


def join(flags, pieces):
    groups, cols, depth = pieces[0].shape
    return pl.pallas_call(
        join_body,
        out_shape=pltpu.VMEM((groups, 4 * cols, depth), bf16),
        in_specs=[SMEM] + [VMEM] * 4,
        out_specs=VMEM,
        cost_estimate=cost(0, 16 * groups * cols * depth),
        compiler_params=grant(10),
        name="join",
    )(flags, *pieces)


def project_body(sizes, ho_ref, w_ref, out_ref, lhs_ref):
    x_size, za_size, zb_size = sizes
    y_size, toks = w_ref.shape[0], ho_ref.shape[1]
    rows = toks // (za_size * zb_size)
    acc = None
    for y in range(y_size):
        for zb in range(zb_size):
            for za in range(za_size):
                for x in range(x_size):
                    at = ((zb * za_size + za) * x_size + x) * rows
                    src = (za * zb_size + zb) * rows
                    lhs_ref[at : at + rows] = ho_ref[x * y_size + y, src : src + rows]
        d = lax.dot_general(
            w_ref[y], lhs_ref[...], (((1,), (1,)), ((), ())), preferred_element_type=f32
        )
        acc = d if acc is None else acc + d
    acc = acc.astype(bf16)
    width = out_ref.shape[2]
    for zb in range(zb_size):
        out_ref[zb] = acc[:, zb * width : (zb + 1) * width]


def project(ho, w, x_size, za_size, zb_size):
    members, toks, depth = ho.shape
    cols = w.shape[1]
    lhs_rows = x_size * toks
    return pl.pallas_call(
        functools.partial(project_body, (x_size, za_size, zb_size)),
        out_shape=jax.ShapeDtypeStruct((zb_size, cols, lhs_rows // zb_size), bf16),
        in_specs=[VMEM, VMEM],
        out_specs=VMEM,
        scratch_shapes=[pltpu.VMEM((lhs_rows, depth), bf16)],
        cost_estimate=cost(2 * members * toks * depth * cols, 2 * members * toks * depth),
        compiler_params=grant(12),
        name="project",
    )(ho, w)


def layer(q_nope, q_rope, w_uk, w_uv, w_o, cache_kv, new_kv, block_order, cache_lengths):
    tok_rows, heads_here, nope_width = q_nope.shape
    latent_width = w_uk.shape[2]
    x_size, zh_size, core_size, za_size, zb_size, y_size = (
        lax.axis_size(a) for a in ("x", "zh", "core", "za", "zb", "y")
    )
    x_at, zh_at, core_at, y_at = (lax.axis_index(a) for a in ("x", "zh", "core", "y"))
    scale = float(nope_width + q_rope.shape[2]) ** (-0.5) * 1.4426950408889634

    own, quarter = pack(cache_kv.T, new_kv.T, latent_width, y_at, y_size)
    line = zh_size * za_size * zb_size
    mirror = [(i, line - 1 - i) for i in range(line)]
    far_quarter = lax.ppermute(quarter, ("zh", "za", "zb"), mirror)

    value_rows, col_count = w_o.shape
    cols = col_count // y_size
    w_t = w_o.T.reshape(y_size, cols, value_rows)
    w_t = lax.all_to_all(w_t, "y", 0, 0, tiled=False)
    near_from = [x_at]
    near = [own]
    for k in (1, x_size - 1, *range(2, x_size - 1)):
        near.append(lax.ppermute(own, "x", [(i, (i + k) % x_size) for i in range(x_size)]))
        near_from.append((x_at - k) % x_size)
    near = jnp.stack(near)
    far = spread(far_quarter, ("x", "y"))
    far = far.reshape(x_size, -1, tok_rows)
    w_far = lax.ppermute(w_t, "zh", swap)
    near_other = lax.ppermute(near, "core", swap)
    far_other = lax.ppermute(far, "core", swap)
    w_other = lax.ppermute(w_t, "core", swap)
    w_far_other = lax.ppermute(w_far, "core", swap)

    ql = jnp.einsum("thn,hnc->htc", q_nope, w_uk, preferred_element_type=f32).astype(bf16)
    ql = ql.reshape(heads_here * tok_rows, latent_width)
    rope = jnp.transpose(q_rope, (1, 0, 2))
    blank = jnp.zeros_like(rope)
    qr = jnp.stack([jnp.concatenate([rope, blank], axis=2), jnp.concatenate([blank, rope], axis=2)])
    qr = qr.reshape(2, heads_here * tok_rows, -1)
    ctx_count = x_size * zh_size * core_size
    shard_ids = jnp.arange(ctx_count, dtype=jnp.int32)
    own_ctx = (x_at * zh_size + zh_at) * core_size + core_at
    own_block = jnp.sum(jnp.where(shard_ids == own_ctx, block_order, 0))

    near_x = jnp.repeat(jnp.stack(near_from), tok_rows, total_repeat_length=x_size * tok_rows)
    far_x = jnp.arange(x_size * tok_rows, dtype=jnp.int32) // tok_rows

    def of_piece(zh_flip, core_flip):
        column = far_x if zh_flip else near_x
        owner = (column * zh_size + (zh_at ^ zh_flip)) * core_size + (core_at ^ core_flip)
        hit = owner[:, None] == shard_ids[None, :]
        limit = jnp.sum(jnp.where(hit, cache_lengths[None, :], 0), axis=1)
        block = jnp.sum(jnp.where(hit, block_order[None, :], 0), axis=1)
        return limit, (block - own_block) * tok_rows

    tables = [of_piece(a, b) for a in range(2) for b in range(2)]
    limits = jnp.stack([t[0] for t in tables])
    where = jnp.stack([t[1] for t in tables])

    pair = (near, near_other)
    state = attend(ql, qr, limits[:2], where[:2], pair, scale, heads_here)
    state = attend(ql, qr, limits[2:3], where[2:3], (far,), scale, heads_here, state)
    head_out = attend(
        ql, qr, limits[3:], where[3:], (far_other,), scale, heads_here, state, w_uv, x_size * y_size
    )

    gathered = lax.all_to_all(head_out, ("x", "y"), 0, 0, tiled=False)
    flags = jnp.stack([zh_at, core_at]).astype(jnp.int32)
    w_all = join(flags, (w_t, w_far, w_other, w_far_other))
    partial = project(gathered, w_all, x_size, za_size, zb_size)

    rows_out = tok_rows // (za_size * zb_size * y_size)
    width = partial.shape[1]
    got = lax.all_to_all(partial, "zb", 0, 0, tiled=False)
    partial = jnp.sum(got.astype(f32), axis=0).astype(bf16).T
    partial = partial.reshape(za_size * x_size * y_size, rows_out, width)
    got = lax.all_to_all(partial, ("za", "x", "y"), 0, 0, tiled=False)
    got = got.reshape(za_size, x_size, y_size, rows_out, zh_size * core_size, cols)
    mixed = jnp.sum(got.astype(f32), axis=0).astype(bf16)
    mixed = jnp.transpose(mixed, (2, 0, 3, 1, 4))
    return mixed.reshape(rows_out, -1)


def solution(mesh):
    axes = ("x", "zh", "core", "za", "zb", "y")
    fine = Mesh(mesh.devices.reshape(4, 2, 2, 2, 4, 4), axes)
    ctx, head = axes[:3], axes[3:]
    in_specs = (
        P(ctx, head, None),
        P(ctx, head, None),
        P(head, None, None),
        P(head, None, None),
        P(head, ctx),
        P(ctx, None),
        P(ctx, None),
        P(),
        P(),
    )
    out_specs = P(axes, None)
    return jax.shard_map(layer, mesh=fine, in_specs=in_specs, out_specs=out_specs, check_vma=False)
```
